128 devices in a mesh: dp: 8 (over z, core), vocab: 16 (over y, x).
Axes of the slice: x: 4, y: 4, z: 4, core: 2. Of those that a mesh axis runs over, the one named last changes fastest.
Arguments:
- hidden: bfloat16 [12288, 896], P(('dp', 'vocab')), may hold values from -400 to 400
- target_ids: int32 [12288], P('dp'), may hold values from 0 to 151935
- owner: int32 [8, 48], P('dp'), may hold values from 0 to 47, each once within a row
- head: bfloat16 [896, 151936], P(None, 'vocab'), may hold values from -0.1875 to 0.1875
Outputs:
- owned_loss: float32 [384, 32], P(('dp', 'vocab'))
The draws below stay inside these ranges and needn't reach their ends.
Inputs may be any that keep to these rules, and one draw needn't show every extreme that they name: Each row of owner names every slot once.
All inputs are finite; a program needn't handle non-finite values.
Results may differ from the reference program's by a relative error of at most 0.0003.
Values may be sent and summed in bfloat16 or wider, within the bound.
A program may use at most 128 MiB of HBM per device.

```python
import math
import jax
import jax.numpy as jnp
import numpy as np
from jax import lax

D = 896
V = 151936
LEN = 32
SEQ_G = 48
TOKENS = 12288
N_DP = 8


def draw_hidden(key, part):
    key_rows, key_scale = jax.random.split(jax.random.fold_in(key, 11), 2)
    noise = jnp.clip(jax.random.normal(key_rows, (TOKENS, D), jnp.float32), -6.0, 6.0)
    scales = 1.5 * jnp.exp(jax.random.uniform(key_scale, (TOKENS, 1), jnp.float32, 0.0, jnp.log(8.0)))
    values = scales * noise
    return jnp.clip(values, -400.0, 400.0).astype(jnp.bfloat16)


def place_ends(result, key, least, largest):
    shape = result.shape
    place = [jax.random.randint(jax.random.fold_in(key, axis), (), 0, shape[axis]) for axis in range(len(shape))]
    result = result.at[tuple(place)].set(least)
    longest = shape.index(max(shape))
    place[longest] = (place[longest] + 1) % shape[longest]
    return result.at[tuple(place)].set(largest)


def shard_levels(stream_key, extent, cuts, least, high):
    gain, own = 1.0, jax.random.fold_in(stream_key, 6)
    for axis_at, blocks in cuts:
        steps = jnp.exp(jax.random.uniform(jax.random.fold_in(own, axis_at), (blocks,), jnp.float32, least / len(cuts), high / len(cuts)))
        gain = gain * jnp.repeat(steps, extent[axis_at] // blocks).reshape([-1 if axis == axis_at else 1 for axis in range(len(extent))])
    return gain


def wide_ids(own_key, extent, amount, slope):
    portions = [min(1 << octave, amount + 1 - (1 << octave)) * (1 << 20) // math.isqrt((1 << octave) ** slope) + 1 for octave in range((amount + 1).bit_length()) if 1 << octave <= amount]
    deviation = 1 + sum(portions) // (1 << 30)
    listing = np.cumsum(np.array([max(1, weight // deviation) for weight in portions]))
    ticket = jax.random.randint(jax.random.fold_in(own_key, 1), extent, 0, int(listing[len(portions) - 1]))
    start = jnp.left_shift(1, jnp.searchsorted(jnp.asarray(listing, jnp.int32), ticket, side="right").astype(jnp.int32))
    rank = start - 1 + jax.random.randint(jax.random.fold_in(own_key, 4), extent, 0, 1 << 30) % jnp.minimum(start, amount + 1 - start)
    return jax.random.permutation(jax.random.fold_in(own_key, 2), amount)[rank].astype(jnp.int32)


def scatter_about(own_key, dims, scale, bound, shards=(), kind=jnp.bfloat16):
    entries = jax.random.normal(own_key, dims, jnp.float32) * scale
    if len(shards) > 0:
        entries = shard_levels(own_key, dims, shards, -0.22, 0.18) * entries
    return jnp.clip(entries, min=-bound, max=bound).astype(kind)


def setup_inputs(seed: int = 0) -> dict:
    streams_of = jax.random.split(jax.random.key(seed), 5)
    return {
        "hidden": draw_hidden(jax.random.fold_in(streams_of[4], 71), 0),
        "target_ids": place_ends(wide_ids(streams_of[1], (TOKENS,), V, 2), jax.random.fold_in(streams_of[1], 3), 0, V - 1).astype(jnp.int32),
        "owner": jax.vmap(lambda own: jax.random.permutation(own, SEQ_G))(jax.random.split(streams_of[2], N_DP)).reshape((N_DP, SEQ_G)).astype(jnp.int32),
        "head": scatter_about(streams_of[3], (D, V), D ** -0.5, 0.1875, ((1, 16),)),
    }


def token_losses(rows, labels, head):
    logits = jnp.dot(rows, head, preferred_element_type=jnp.float32)
    peak = jnp.max(logits, axis=1)
    expsum = jnp.sum(jnp.exp(logits - peak[:, None]), axis=1)
    column = lax.broadcasted_iota(jnp.int32, logits.shape, 1)
    picked = jnp.sum(jnp.where(column == labels.astype(jnp.int32)[:, None], logits, jnp.zeros_like(logits)), axis=1)
    return peak + jnp.log(expsum) - picked


def reference(hidden, target_ids, owner, head):
    count = hidden.shape[0]
    step_rows = math.gcd(count, 512)
    blocks = (hidden.reshape(count // step_rows, step_rows, hidden.shape[1]), target_ids.reshape(count // step_rows, step_rows))
    losses = lax.map(lambda pair: token_losses(pair[0], pair[1], head), blocks)
    losses = losses.reshape(N_DP, SEQ_G, LEN)
    groups = jnp.arange(N_DP, dtype=jnp.int32)[:, None]
    placed = jnp.zeros_like(losses).at[groups, owner.astype(jnp.int32)].set(losses)
    return placed.reshape(N_DP * SEQ_G, LEN)
```

```python
import functools

import jax
import jax.numpy as jnp
from jax import lax
from jax.experimental import pallas as pl
from jax.experimental.pallas import tpu as pltpu
from jax.sharding import PartitionSpec as P

MESH = pl.DeviceIdType.MESH
SIDE = 4
PEERS = SIDE * SIDE
TILE = 256
PAIR = 2 * TILE
LOW = -1e30

OWN = [(0, 0, 0), (0, 0, 1)]
FIRST = [(1, 0, 0), (3, 0, 0), (0, 1, 1), (0, 3, 1)]
SECOND = [(2, 0, 0), (0, 2, 1)]
DIRECT = [(0, 1, 0), (0, 3, 0), (1, 0, 1), (3, 0, 1), (0, 2, 0), (2, 0, 1)]
RELAYED = [
    (dx, dy, half)
    for a, b in ((1, 1), (1, 3), (3, 1), (3, 3), (1, 2), (3, 2), (2, 1), (2, 3), (2, 2))
    for dx, dy, half in ((a, b, 0), (b, a, 1))
]
UNITS = OWN + FIRST + SECOND + DIRECT + RELAYED
SLOT = {unit: i for i, unit in enumerate(UNITS)}


def mult(value, of):
    return value if isinstance(value, int) else pl.multiple_of(value, of)


def kernel(
    hidden_ref, target_ref, owner_ref, head_ref, out_ref,
    xbuf, wbuf, wtail, wpad, tok, lab, peak_ref, sum_ref, pick_ref, flat, ordered, got,
    own_sem, head_sem, send_sem, recv_sem, out_sem, in_sem, entered,
):
    rows_own, depth = hidden_ref.shape
    width = head_ref.shape[1]
    half_rows = rows_own // 2
    count = xbuf.shape[0]
    block = 4 * half_rows
    groups = count // block
    pairs = wbuf.shape[1] // PAIR
    whole = width // PAIR
    edge = width // 128 * 128
    steps = groups * pairs

    me = lax.axis_index("vocab")
    y, x = lax.div(me, SIDE), lax.rem(me, SIDE)

    def at(dx, dy):
        return {"vocab": lax.rem(y + dy, SIDE) * SIDE + lax.rem(x + dx, SIDE)}

    own_copy = pltpu.make_async_copy(hidden_ref, xbuf.at[pl.ds(0, rows_own)], own_sem)
    own_copy.start()

    def head_chunk(i):
        cols = pl.ds(mult(i * PAIR, PAIR), PAIR)
        return pltpu.make_async_copy(head_ref.at[:, cols], wbuf.at[:, cols], head_sem.at[i])

    rest = pl.ds(whole * PAIR, edge - whole * PAIR)
    rest_copy = pltpu.make_async_copy(head_ref.at[:, rest], wbuf.at[:, rest], head_sem.at[whole])
    tail_copy = pltpu.make_async_copy(
        head_ref.at[:, pl.ds(edge, width - edge)], wtail, head_sem.at[whole + 1]
    )
    for i in range(whole):
        head_chunk(i).start()
    rest_copy.start()
    tail_copy.start()

    barrier = pltpu.get_barrier_semaphore()
    for d in (1, 2, 3):
        pl.semaphore_signal(barrier, inc=1, device_id=at(d, 0), device_id_type=MESH)
        pl.semaphore_signal(barrier, inc=1, device_id=at(0, d), device_id_type=MESH)
    pl.semaphore_wait(barrier, 6)

    sends = []

    def send(src, unit, dx, dy):
        there = ((unit[0] - dx) % SIDE, (unit[1] - dy) % SIDE, unit[2])
        slot = SLOT[there]
        copy = pltpu.make_async_remote_copy(
            src_ref=src,
            dst_ref=xbuf.at[pl.ds(slot * half_rows, half_rows)],
            send_sem=send_sem.at[len(sends)],
            recv_sem=recv_sem.at[slot],
            device_id=at(dx, dy),
            device_id_type=MESH,
        )
        copy.start()
        sends.append(unit)

    def arrived(slot):
        here = xbuf.at[pl.ds(mult(slot * half_rows, half_rows), half_rows)]
        pltpu.make_async_remote_copy(
            src_ref=here, dst_ref=here, send_sem=send_sem.at[0], recv_sem=recv_sem.at[slot],
            device_id=at(1, 0), device_id_type=MESH,
        ).wait_recv()

    def piece(unit):
        return xbuf.at[pl.ds(SLOT[unit] * half_rows, half_rows)]

    mine = [hidden_ref.at[pl.ds(h * half_rows, half_rows)] for h in (0, 1)]
    for d in (1, 3, 2):
        send(mine[0], OWN[0], d, 0)
        send(mine[1], OWN[1], 0, d)
    for d in (1, 3, 2):
        send(mine[0], OWN[0], 0, d)
        send(mine[1], OWN[1], d, 0)
    for d in (1, 2, 3):
        pl.semaphore_signal(entered, inc=1, device_id=at(0, d), device_id_type=MESH)

    lane = lax.broadcasted_iota(jnp.int32, (128, 128), 1)
    base = me * width
    for i in range(count // 128):
        ids = jnp.broadcast_to(target_ref[i : i + 1, :], (128, 128)).T - base
        tok[i * 128 : (i + 1) * 128, :] = (
            jnp.where((ids >= 0) & (ids < width), ids, -(1 << 24)) - lane
        )

    def place(unit):
        dx, dy, half = unit
        source = lax.rem(y + dy, SIDE) * SIDE + lax.rem(x + dx, SIDE)
        return mult(source * rows_own + half * half_rows, half_rows)

    for i, unit in enumerate(UNITS):
        lab[i * half_rows : (i + 1) * half_rows, :] = tok[pl.ds(place(unit), half_rows), :]
    peak_ref[...] = jnp.full_like(peak_ref, LOW)
    sum_ref[...] = jnp.zeros_like(sum_ref)
    pick_ref[...] = jnp.zeros_like(pick_ref)
    wpad[...] = jnp.zeros_like(wpad)
    ahead = whole * PAIR
    over = lax.broadcasted_iota(jnp.int32, (16, wbuf.shape[1] - ahead), 1) + ahead >= width
    top_row = lax.broadcasted_iota(jnp.int32, (16, wbuf.shape[1] - ahead), 0) == 0
    wpad[:, ahead:] = jnp.where(over & top_row, LOW, 0.0).astype(jnp.bfloat16)
    wbuf[:, edge:] = jnp.zeros((depth, wbuf.shape[1] - edge), jnp.bfloat16)

    own_copy.wait()
    for unit in FIRST:
        arrived(SLOT[unit])
        for d in (1, 3, 2):
            send(piece(unit), unit, *((0, d) if unit[2] == 0 else (d, 0)))

    def multiply(*accs):
        acc = [[accs[0], accs[1]], [accs[2], accs[3]]]
        last = depth // TILE
        left = depth - last * TILE
        ones = (lax.broadcasted_iota(jnp.int32, (block, TILE - left), 1) == 0).astype(jnp.float32)
        ones = ones.astype(jnp.bfloat16)

        def push(k, c, reg):
            for u in range(2):
                cols = pl.ds(mult(c + u * TILE, TILE), TILE)
                if k < last:
                    rhs = wbuf[k * TILE : (k + 1) * TILE, cols]
                else:
                    fill = jnp.zeros((TILE - left - 16, TILE), jnp.bfloat16)
                    rhs = jnp.concatenate([wbuf[k * TILE :, cols], wpad[:, cols], fill], axis=0)
                pltpu.matmul_push_rhs(rhs, reg, u)

        def where_is(n):
            g = n // pairs if isinstance(n, int) else lax.div(n, pairs)
            return mult(g * block, block), mult((n - g * pairs) * PAIR, PAIR)

        def mm(r, c, after, slot):
            for k in range(last + 1):
                if k < last:
                    push(k + 1, c, (k + 1) % 2)
                    lhs = xbuf[pl.ds(r, block), k * TILE : (k + 1) * TILE]
                else:
                    push(0, after, (k + 1) % 2)
                    lhs = jnp.concatenate([xbuf[pl.ds(r, block), k * TILE :], ones], axis=1)
                for u in range(2):
                    pltpu.matmul_acc_lhs(acc[u][slot], lhs, load_staged_rhs=k % 2)

        def statistics(r, c, slot):
            rows = pl.ds(r, block)
            a, b = pltpu.matmul_pop(acc[0][slot]), pltpu.matmul_pop(acc[1][slot])
            logits = [a[:, :128], a[:, 128:], b[:, :128], b[:, 128:]]
            label = lab[rows, :] - c
            old, total, picked = peak_ref[rows, :], sum_ref[rows, :], pick_ref[rows, :]
            peak = old
            for v in logits:
                peak = jnp.maximum(peak, v)
            total = total * jnp.exp(old - peak)
            for v in logits:
                total = total + jnp.exp(v - peak)
            for i, v in enumerate(logits):
                picked = jnp.where(label == i * 128, v, picked)
            peak_ref[rows, :], sum_ref[rows, :], pick_ref[rows, :] = peak, total, picked

        head_chunk(0).wait()
        head_chunk(1).wait()
        push(0, 0, 0)
        mm(*where_is(0), PAIR, 0)

        def arrivals(q, g, lo, hi):
            first = (g * pairs - 1) // 2

            @pl.when(q == first)
            def _():
                if g == 1:
                    for unit in SECOND:
                        arrived(SLOT[unit])
                        for d in (1, 3, 2):
                            send(piece(unit), unit, *((0, d) if unit[2] == 0 else (d, 0)))
                else:

                    @pl.loop(lo, hi)
                    def _(slot):
                        arrived(slot)

        @pl.loop(0, (steps - 2) // 2)
        def _(q):
            @pl.when(q < (whole - 2) // 2)
            def _():
                head_chunk(2 * q + 2).wait()
                head_chunk(2 * q + 3).wait()

            @pl.when(q == (whole - 2) // 2)
            def _():
                rest_copy.wait()
                tail_copy.wait()
                wbuf[:, edge : edge + 128] = jnp.concatenate(
                    [wtail[...], jnp.zeros((depth, 128 - (width - edge)), jnp.bfloat16)], axis=1
                )

            for g in range(1, groups):
                arrivals(q, g, g * 4, g * 4 + 4)
            spots = [where_is(2 * q + j) for j in range(4)]
            for j in range(2):
                mm(*spots[j + 1], spots[j + 2][1], (j + 1) % 2)
                statistics(*spots[j], j % 2)

        before, final = where_is(steps - 2), where_is(steps - 1)
        mm(*final, 0, 1)
        statistics(*before, 0)
        for u in range(2):
            pltpu.matmul_acc_lhs(acc[u][0], jnp.zeros((block, TILE), jnp.bfloat16), load_staged_rhs=0)
        statistics(*final, 1)
        for u in range(2):
            pltpu.matmul_pop(acc[u][0])

    pl.run_scoped(multiply, *[pltpu.ACC(u)((block, TILE), jnp.float32) for u in (0, 0, 1, 1)])

    seq_count = owner_ref.shape[1]
    length = count // seq_count
    lanes = lax.broadcasted_iota(jnp.int32, (half_rows, 128), 1)
    for i, unit in enumerate(UNITS):
        rows = slice(i * half_rows, (i + 1) * half_rows)
        peak = jnp.max(peak_ref[rows, :], axis=1, keepdims=True)
        total = jnp.sum(sum_ref[rows, :] * jnp.exp(peak_ref[rows, :] - peak), axis=1, keepdims=True)
        picked = jnp.sum(pick_ref[rows, :], axis=1, keepdims=True)
        flat[pl.ds(place(unit), half_rows), :] = jnp.where(
            lanes < length, peak, jnp.where(lanes < 2 * length, total, picked)
        )
    spot = lax.broadcasted_iota(jnp.int32, (count, 128), 0) % length
    lanes = lax.broadcasted_iota(jnp.int32, (count, 128), 1)
    by_token = jnp.where((lanes % length == spot) & (lanes < 3 * length), flat[...], 0.0)
    by_seq = jnp.sum(by_token.reshape(seq_count, length, 128), axis=1)
    owned = seq_count // PEERS
    row = lax.broadcasted_iota(jnp.int32, (8 * PEERS, 128), 0)
    slot_of = jnp.where(row % 8 < owned, row // 8 * owned + row % 8, -1)
    sorted_rows = jnp.zeros((8 * PEERS, 128), jnp.float32)
    for i in range(seq_count):
        owner = jnp.broadcast_to(owner_ref[:, i : i + 1], (1, 128))
        sorted_rows = jnp.where(slot_of == owner, by_seq[i : i + 1, :], sorted_rows)
    ordered[...] = sorted_rows

    pl.semaphore_wait(entered, 3)
    outs = []
    for d in range(1, PEERS):
        to = lax.rem(me + d, PEERS)
        copy = pltpu.make_async_remote_copy(
            src_ref=ordered.at[pl.ds(mult(to * 8, 8), 8)],
            dst_ref=got.at[d],
            send_sem=out_sem.at[d],
            recv_sem=in_sem.at[d],
            device_id={"vocab": to},
            device_id_type=MESH,
        )
        copy.start()
        outs.append(copy)
    got[0] = ordered[pl.ds(mult(me * 8, 8), 8), :]
    for copy in outs:
        copy.wait_recv()
    top = got[0]
    for d in range(1, PEERS):
        top = jnp.maximum(top, got[d])
    total, picked = jnp.zeros_like(top), jnp.zeros_like(top)
    for d in range(PEERS):
        scale = pltpu.roll(jnp.exp(got[d] - top), length, 1)
        total = total + got[d] * scale
        picked = picked + got[d]
    loss = top[:, :length] + jnp.log(total[:, length : 2 * length]) - picked[:, 2 * length : 3 * length]
    out_ref[...] = loss[:owned, :]
    for i, unit in enumerate(sends):
        pltpu.make_async_remote_copy(
            src_ref=piece(unit), dst_ref=piece(unit), send_sem=send_sem.at[i], recv_sem=recv_sem.at[0],
            device_id=at(1, 0), device_id_type=MESH,
        ).wait_send()
    for copy in outs:
        copy.wait_send()


def local(hidden, target_ids, owner, head):
    rows_own, depth = hidden.shape
    count = target_ids.shape[0]
    width = head.shape[1]
    wide = -(-width // PAIR) * PAIR
    seq_count = owner.shape[1]
    length = count // seq_count
    vmem = pl.BlockSpec(memory_space=pltpu.VMEM)
    anywhere = pl.BlockSpec(memory_space=pl.ANY)
    stat = pltpu.VMEM((count, 128), jnp.float32)
    return pl.pallas_call(
        kernel,
        out_shape=jax.ShapeDtypeStruct((seq_count // PEERS, length), jnp.float32),
        in_specs=[anywhere, vmem, vmem, anywhere],
        out_specs=vmem,
        scratch_shapes=[
            pltpu.VMEM((count, depth), jnp.bfloat16),
            pltpu.VMEM((depth, wide), jnp.bfloat16),
            pltpu.VMEM((depth, width % 128), jnp.bfloat16),
            pltpu.VMEM((16, wide), jnp.bfloat16),
            pltpu.VMEM((count, 128), jnp.int32),
            pltpu.VMEM((count, 128), jnp.int32),
            stat, stat, stat, stat,
            pltpu.VMEM((8 * PEERS, 128), jnp.float32),
            pltpu.VMEM((PEERS, 8, 128), jnp.float32),
            pltpu.SemaphoreType.DMA,
            pltpu.SemaphoreType.DMA((width // PAIR + 2,)),
            pltpu.SemaphoreType.DMA((len(UNITS),)),
            pltpu.SemaphoreType.DMA((len(UNITS),)),
            pltpu.SemaphoreType.DMA((PEERS,)),
            pltpu.SemaphoreType.DMA((PEERS,)),
            pltpu.SemaphoreType.REGULAR,
        ],
        compiler_params=pltpu.CompilerParams(collective_id=0, has_side_effects=True),
    )(hidden, target_ids.reshape(count // 128, 128), owner, head)


def solution(mesh):
    return jax.shard_map(
        local,
        mesh=mesh,
        in_specs=(P(("dp", "vocab"), None), P("dp"), P("dp", None), P(None, "vocab")),
        out_specs=P(("dp", "vocab"), None),
        check_vma=False,
    )
```

```python
import jax
import jax.numpy as jnp
from jax import lax
from jax.experimental import pallas as pl
from jax.experimental.pallas import tpu as pltpu
from jax.sharding import PartitionSpec as P

MESH = pl.DeviceIdType.MESH
SIDE = 4
PEERS = SIDE * SIDE
TILE = 256
CHUNK = 432
GROUP = 9
LOW = -1e30

OWN = [(0, 0, 0), (0, 0, 1)]
FIRST = [(1, 0, 0), (3, 0, 0), (0, 1, 1), (0, 3, 1)]
SECOND = [(2, 0, 0), (0, 2, 1)]
DIRECT = [(0, 1, 0), (0, 3, 0), (1, 0, 1), (3, 0, 1), (0, 2, 0), (2, 0, 1)]
RELAYED = [
    (dx, dy, half)
    for a, b in ((1, 1), (1, 3), (3, 1), (3, 3), (1, 2), (3, 2), (2, 1), (2, 3), (2, 2))
    for dx, dy, half in ((a, b, 0), (b, a, 1))
]
UNITS = OWN + FIRST + SECOND + DIRECT + RELAYED
SLOT = {unit: i for i, unit in enumerate(UNITS)}


def mult(value, of):
    return value if isinstance(value, int) else pl.multiple_of(value, of)


def kernel(
    hidden_ref, target_ref, owner_ref, head_ref, out_ref,
    xbuf, wbuf, low, tok, lab, peak_ref, sum_ref, pick_ref, flat, ordered, got,
    own_sem, head_sem, send_sem, recv_sem, out_sem, in_sem, entered,
):
    rows_own, depth = hidden_ref.shape
    width = head_ref.shape[0]
    half_rows = rows_own // 2
    count = xbuf.shape[0]
    tiles = count // TILE
    both = 2 * CHUNK
    per_tile = wbuf.shape[0] // both
    steps = tiles * per_tile
    last_rows = width - (per_tile - 1) * both

    me = lax.axis_index("vocab")
    y, x = lax.div(me, SIDE), lax.rem(me, SIDE)

    def at(dx, dy):
        return {"vocab": lax.rem(y + dy, SIDE) * SIDE + lax.rem(x + dx, SIDE)}

    own_copy = pltpu.make_async_copy(hidden_ref, xbuf.at[pl.ds(0, rows_own)], own_sem)
    own_copy.start()

    def head_chunk(i, rows=both):
        part = pl.ds(mult(i * both, 16), rows)
        return pltpu.make_async_copy(head_ref.at[part], wbuf.at[part], head_sem.at[i])

    for i in range(per_tile - 1):
        head_chunk(i).start()
    head_chunk(per_tile - 1, last_rows).start()

    barrier = pltpu.get_barrier_semaphore()
    for d in (1, 2, 3):
        pl.semaphore_signal(barrier, inc=1, device_id=at(d, 0), device_id_type=MESH)
        pl.semaphore_signal(barrier, inc=1, device_id=at(0, d), device_id_type=MESH)
    pl.semaphore_wait(barrier, 6)

    sends = []

    def send(src, unit, dx, dy):
        there = ((unit[0] - dx) % SIDE, (unit[1] - dy) % SIDE, unit[2])
        slot = SLOT[there]
        copy = pltpu.make_async_remote_copy(
            src_ref=src,
            dst_ref=xbuf.at[pl.ds(slot * half_rows, half_rows)],
            send_sem=send_sem.at[len(sends)],
            recv_sem=recv_sem.at[slot],
            device_id=at(dx, dy),
            device_id_type=MESH,
        )
        copy.start()
        sends.append(unit)

    def arrived(slot):
        here = xbuf.at[pl.ds(mult(slot * half_rows, half_rows), half_rows)]
        pltpu.make_async_remote_copy(
            src_ref=here, dst_ref=here, send_sem=send_sem.at[0], recv_sem=recv_sem.at[slot],
            device_id=at(1, 0), device_id_type=MESH,
        ).wait_recv()

    def piece(unit):
        return xbuf.at[pl.ds(SLOT[unit] * half_rows, half_rows)]

    mine = [hidden_ref.at[pl.ds(h * half_rows, half_rows)] for h in (0, 1)]
    for d in (1, 3, 2):
        send(mine[0], OWN[0], d, 0)
        send(mine[1], OWN[1], 0, d)
    for d in (1, 3, 2):
        send(mine[0], OWN[0], 0, d)
        send(mine[1], OWN[1], d, 0)
    for d in (1, 2, 3):
        pl.semaphore_signal(entered, inc=1, device_id=at(0, d), device_id_type=MESH)

    lane = lax.broadcasted_iota(jnp.int32, (8, 128), 1)
    sub = lax.broadcasted_iota(jnp.int32, (8, 128), 0)

    def window(rows, start):
        a, o = divmod(start, 128)
        part = rows[a]
        if o:
            part = pltpu.roll(part, 128 - o, 1)
            if o + half_rows > 128:
                part = jnp.where(lane < 128 - o, part, pltpu.roll(rows[a + 1], 128 - o, 1))
        return part

    def source(unit):
        dx, dy, _ = unit
        return lax.rem(y + dy, SIDE) * SIDE + lax.rem(x + dx, SIDE)

    ids = [jnp.broadcast_to(target_ref[i : i + 1, :], (8, 128)) for i in range(count // 128)]
    for i in range(2 * PEERS):
        tok[i] = window(ids, i * half_rows)
    base = me * width
    for w in range(count // 128):
        label = jnp.zeros((8, 128), jnp.int32)
        for i in range(128 * w // half_rows, (128 * w + 127) // half_rows + 1):
            start = half_rows * i - 128 * w
            part = tok[source(UNITS[i]) * 2 + UNITS[i][2]]
            if start % 128:
                part = pltpu.roll(part, start % 128, 1)
            label = part if start <= 0 else jnp.where(lane < start, label, part)
        label = label - base
        label = jnp.where((label >= 0) & (label < width), label, -(1 << 24)) - sub
        lab[w // 2, :, (w % 2) * 128 : (w % 2 + 1) * 128] = label
    peak_ref[...] = jnp.full_like(peak_ref, LOW)
    sum_ref[...] = jnp.zeros_like(sum_ref)
    pick_ref[...] = jnp.zeros_like(pick_ref)
    spare = wbuf.shape[0] - width
    wbuf[width:, :] = jnp.zeros((spare, depth), jnp.bfloat16)
    low_row = lax.broadcasted_iota(jnp.int32, (32, 128), 0) >= 32 - spare
    low_lane = lax.broadcasted_iota(jnp.int32, (32, 128), 1) == 0
    low[...] = jnp.where(low_row & low_lane, LOW, 0.0).astype(jnp.bfloat16)

    own_copy.wait()
    for unit in FIRST:
        arrived(SLOT[unit])
        for d in (1, 3, 2):
            send(piece(unit), unit, *((0, d) if unit[2] == 0 else (d, 0)))

    def multiply(*accs):
        acc = [[accs[0], accs[1]], [accs[2], accs[3]]]
        last = depth // TILE
        left = TILE - (depth - last * TILE)
        ones = (lax.broadcasted_iota(jnp.int32, (TILE, left), 1) == 0).astype(jnp.float32)
        ones = ones.astype(jnp.bfloat16)

        def push(k, t, reg):
            tokens = pl.ds(mult(t * TILE, TILE), TILE)
            if k < last:
                held = xbuf[tokens, k * TILE : (k + 1) * TILE]
            else:
                held = jnp.concatenate([xbuf[tokens, k * TILE :], ones], axis=1)
            for u in range(2):
                pltpu.matmul_push_rhs(held, reg, u, transpose=True)

        def where_is(n):
            t = n // per_tile if isinstance(n, int) else lax.div(n, per_tile)
            return t, n - t * per_tile

        def mm(t, s, after, slot):
            for k in range(last + 1):
                if k < last:
                    push(k + 1, t, (k + 1) % 2)
                else:
                    push(0, after, (k + 1) % 2)
                for u in range(2):
                    rows = pl.ds(mult(s * both + u * CHUNK, 16), CHUNK)
                    if k < last:
                        lhs = wbuf[rows, k * TILE : (k + 1) * TILE]
                    else:
                        pad = jnp.zeros((CHUNK, left), jnp.bfloat16)
                        if u == 1:
                            end = s // (per_tile - 1) if isinstance(s, int) else lax.div(s, per_tile - 1)
                            pad = jnp.concatenate([pad[16:], low[pl.ds(mult(end * 16, 16), 16), :]], axis=0)
                        lhs = jnp.concatenate([wbuf[rows, k * TILE :], pad], axis=1)
                    pltpu.matmul_acc_lhs(acc[u][slot], lhs, load_staged_rhs=k % 2)

        def statistics(t, s, slot):
            picked = pick_ref[t]
            for u in range(2):
                logits = pltpu.matmul_pop(acc[u][slot])
                label = lab[t] - (s * both + u * CHUNK)
                peak, total = peak_ref[t, u], sum_ref[t, u]
                for g in range(0, CHUNK // 8, GROUP):
                    part = [logits[j * 8 : (j + 1) * 8, :] for j in range(g, g + GROUP)]
                    top = part[0]
                    for v in part[1:]:
                        top = jnp.maximum(top, v)
                    old, peak = peak, jnp.maximum(peak, top)
                    terms = [jnp.exp(v - peak) for v in part]
                    while len(terms) > 1:
                        pairs = [a + b for a, b in zip(terms[::2], terms[1::2])]
                        terms = pairs + terms[2 * len(pairs) :]
                    total = total * jnp.exp(old - peak) + terms[0]
                    for i, v in enumerate(part):
                        picked = jnp.where(label == (g + i) * 8, v, picked)
                peak_ref[t, u], sum_ref[t, u] = peak, total
            pick_ref[t] = picked

        head_chunk(0).wait()
        push(0, 0, 0)
        mm(0, 0, 0, 0)

        @pl.loop(0, (steps - 2) // 2)
        def _(q):
            @pl.when(q < (per_tile - 3) // 2)
            def _():
                head_chunk(2 * q + 1).wait()
                head_chunk(2 * q + 2).wait()

            @pl.when(q == (per_tile - 3) // 2)
            def _():
                head_chunk(per_tile - 2).wait()
                head_chunk(per_tile - 1, last_rows).wait()

            for t in range(1, tiles):

                @pl.when(q == (t * per_tile - 2) // 2)
                def _():
                    lo, hi = (-(-TILE * i // half_rows) for i in (t, t + 1))
                    if t == 1:
                        for unit in SECOND:
                            arrived(SLOT[unit])
                            for d in (1, 3, 2):
                                send(piece(unit), unit, *((0, d) if unit[2] == 0 else (d, 0)))
                        lo += len(SECOND)

                    @pl.loop(lo, hi)
                    def _(slot):
                        arrived(slot)

            spots = [where_is(2 * q + j) for j in range(4)]
            for j in range(2):
                mm(*spots[j + 1], spots[j + 2][0], (j + 1) % 2)
                statistics(*spots[j], j % 2)

        before, final = where_is(steps - 2), where_is(steps - 1)
        mm(*final, 0, 1)
        statistics(*before, 0)
        for u in range(2):
            pltpu.matmul_acc_lhs(acc[u][0], jnp.zeros((CHUNK, TILE), jnp.bfloat16), load_staged_rhs=0)
        statistics(*final, 1)
        for u in range(2):
            pltpu.matmul_pop(acc[u][0])

    pl.run_scoped(multiply, *[pltpu.ACC(u)((CHUNK, TILE), jnp.float32) for u in (0, 0, 1, 1)])

    sub_wide = lax.broadcasted_iota(jnp.int32, (8, TILE), 0)
    stats = []
    for t in range(tiles):
        peaks = jnp.concatenate([peak_ref[t, 0], peak_ref[t, 1]], axis=0)
        sums = jnp.concatenate([sum_ref[t, 0], sum_ref[t, 1]], axis=0)
        peak = jnp.max(peaks, axis=0, keepdims=True)
        total = jnp.sum(sums * jnp.exp(peaks - peak), axis=0, keepdims=True)
        picked = jnp.sum(pick_ref[t], axis=0, keepdims=True)
        packed = jnp.where(sub_wide == 0, peak, jnp.where(sub_wide == 1, total, picked))
        stats += [packed[:, i : i + 128] for i in range(0, TILE, 128)]
    for i, unit in enumerate(UNITS):
        flat[unit[2], source(unit)] = window(stats, i * half_rows)
    seq_count = owner_ref.shape[1]
    length = count // seq_count
    owned = seq_count // PEERS
    group = lane // length
    messages = [jnp.zeros((8, 128), jnp.float32) for _ in range(PEERS)]
    for v in range(PEERS):
        merged = jnp.where(lane < half_rows, flat[0, v], pltpu.roll(flat[1, v], half_rows, 1))
        turned = [merged] + [pltpu.roll(merged, i * length, 1) for i in range(1, 128 // length)]
        for j in range(owned):
            row = turned[-j % len(turned)]
            for i in range(1, owned):
                row = jnp.where(group < i, row, turned[(i - j) % len(turned)])
            seq = v * owned + j
            slot = jnp.broadcast_to(owner_ref[:, seq : seq + 1], (8, 128)) - group
            for to in range(PEERS):
                messages[to] = jnp.where(slot == to * owned, row, messages[to])
    for to in range(PEERS):
        ordered[to] = messages[to]

    pl.semaphore_wait(entered, 3)
    outs = []
    for d in range(1, PEERS):
        to = lax.rem(me + d, PEERS)
        copy = pltpu.make_async_remote_copy(
            src_ref=ordered.at[to],
            dst_ref=got.at[d],
            send_sem=out_sem.at[d],
            recv_sem=in_sem.at[d],
            device_id={"vocab": to},
            device_id_type=MESH,
        )
        copy.start()
        outs.append(copy)
    got[0] = ordered[me]
    for copy in outs:
        copy.wait_recv()
    parts = [got[d] for d in range(PEERS)]
    top = parts[0]
    for part in parts[1:]:
        top = jnp.maximum(top, part)
    total, picked = jnp.zeros_like(top), jnp.zeros_like(top)
    for part in parts:
        total = total + part * pltpu.roll(jnp.exp(part - top), 1, 0)
        picked = picked + part
    loss = top[0:1, :] + jnp.log(total[1:2, :]) - picked[2:3, :]
    for i in range(owned):
        out_ref[i : i + 1, :] = loss[:, i * length : (i + 1) * length]
    for i, unit in enumerate(sends):
        pltpu.make_async_remote_copy(
            src_ref=piece(unit), dst_ref=piece(unit), send_sem=send_sem.at[i], recv_sem=recv_sem.at[0],
            device_id=at(1, 0), device_id_type=MESH,
        ).wait_send()
    for copy in outs:
        copy.wait_send()


def local(hidden, target_ids, owner, head):
    depth = hidden.shape[1]
    count = target_ids.shape[0]
    rows = head.shape[1]
    tall = -(-rows // (2 * CHUNK)) * 2 * CHUNK
    seq_count = owner.shape[1]
    tiles = count // TILE
    vmem = pl.BlockSpec(memory_space=pltpu.VMEM)
    anywhere = pl.BlockSpec(memory_space=pl.ANY)
    f32 = jnp.float32
    return pl.pallas_call(
        kernel,
        out_shape=jax.ShapeDtypeStruct((seq_count // PEERS, count // seq_count), f32),
        in_specs=[anywhere, vmem, vmem, anywhere],
        out_specs=vmem,
        scratch_shapes=[
            pltpu.VMEM((count, depth), jnp.bfloat16),
            pltpu.VMEM((tall, depth), jnp.bfloat16),
            pltpu.VMEM((32, 128), jnp.bfloat16),
            pltpu.VMEM((2 * PEERS, 8, 128), jnp.int32),
            pltpu.VMEM((tiles, 8, TILE), jnp.int32),
            pltpu.VMEM((tiles, 2, 8, TILE), f32),
            pltpu.VMEM((tiles, 2, 8, TILE), f32),
            pltpu.VMEM((tiles, 8, TILE), f32),
            pltpu.VMEM((2, PEERS, 8, 128), f32),
            pltpu.VMEM((PEERS, 8, 128), f32),
            pltpu.VMEM((PEERS, 8, 128), f32),
            pltpu.SemaphoreType.DMA,
            pltpu.SemaphoreType.DMA((tall // (2 * CHUNK),)),
            pltpu.SemaphoreType.DMA((len(UNITS),)),
            pltpu.SemaphoreType.DMA((len(UNITS),)),
            pltpu.SemaphoreType.DMA((PEERS,)),
            pltpu.SemaphoreType.DMA((PEERS,)),
            pltpu.SemaphoreType.REGULAR,
        ],
        compiler_params=pltpu.CompilerParams(
            collective_id=0,
            has_side_effects=True,
        ),
    )(hidden, target_ids.reshape(count // 128, 128), owner, head.T)


def solution(mesh):
    return jax.shard_map(
        local,
        mesh=mesh,
        in_specs=(P(("dp", "vocab"), None), P("dp"), P("dp", None), P(None, "vocab")),
        out_specs=P(("dp", "vocab"), None),
        check_vma=False,
    )
```

```python
import jax
import jax.numpy as jnp
from jax import lax
from jax.experimental import pallas as pl
from jax.experimental.pallas import tpu as pltpu
from jax.sharding import PartitionSpec as P

MESH = pl.DeviceIdType.MESH
SIDE = 4
PEERS = SIDE * SIDE
TILE = 256
CHUNK = 432
GROUP = 9
LOW = -1e30

UNITS = [
    (0, 0, 0), (0, 0, 1), (1, 0, 0), (3, 0, 0), (0, 1, 1), (0, 3, 1),
    (2, 0, 0), (0, 2, 1), (0, 1, 0), (1, 0, 1), (0, 3, 0),
    (3, 0, 1), (1, 3, 0), (3, 1, 1), (3, 3, 0), (3, 3, 1),
    (1, 1, 0), (1, 1, 1), (3, 1, 0), (1, 3, 1), (2, 1, 0), (1, 2, 1),
    (0, 2, 0), (2, 0, 1), (2, 3, 0), (3, 2, 1), (1, 2, 0),
    (2, 1, 1), (3, 2, 0), (2, 3, 1), (2, 2, 0), (2, 2, 1),
]
SLOT = {unit: i for i, unit in enumerate(UNITS)}


def mult(value, of):
    return value if isinstance(value, int) else pl.multiple_of(value, of)


def onward(unit):
    dx, dy, half = unit
    first, second = (dx, dy) if half == 0 else (dy, dx)
    steps = []
    if second == 0:
        if first == 1:
            steps.append((-1, 0))
        steps += [(0, 1), (0, -1)]
    elif second == 1 and first % 2 == 0:
        steps.append((0, -1))
    elif second == 3 and first % 2 == 1:
        steps.append((0, 1))
    return [(i, j) if half == 0 else (j, i) for i, j in steps]


def kernel(
    hidden_ref, target_ref, owner_ref, head_ref, out_ref,
    xbuf, wbuf, low, tok, lab, peak_ref, sum_ref, pick_ref, flat, ordered, got,
    own_sem, head_sem, send_sem, recv_sem, out_sem, in_sem, entered,
):
    rows_own, depth = hidden_ref.shape
    width = head_ref.shape[0]
    half_rows = rows_own // 2
    count = xbuf.shape[0]
    tiles = count // TILE
    both = 2 * CHUNK
    per_tile = wbuf.shape[0] // both
    steps = tiles * per_tile
    last_rows = width - (per_tile - 1) * both

    me = lax.axis_index("vocab")
    y, x = lax.div(me, SIDE), lax.rem(me, SIDE)

    def at(dx, dy):
        return {"vocab": lax.rem(y + dy, SIDE) * SIDE + lax.rem(x + dx, SIDE)}

    own_copy = pltpu.make_async_copy(hidden_ref, xbuf.at[pl.ds(0, rows_own)], own_sem)
    own_copy.start()

    def head_chunk(i, rows=both):
        part = pl.ds(mult(i * both, 16), rows)
        return pltpu.make_async_copy(head_ref.at[part], wbuf.at[part], head_sem.at[i])

    for i in range(per_tile - 1):
        head_chunk(i).start()
    head_chunk(per_tile - 1, last_rows).start()

    barrier = pltpu.get_barrier_semaphore()
    for d in (1, 2, 3):
        pl.semaphore_signal(barrier, inc=1, device_id=at(d, 0), device_id_type=MESH)
        pl.semaphore_signal(barrier, inc=1, device_id=at(0, d), device_id_type=MESH)
    pl.semaphore_wait(barrier, 6)

    sends = []

    def send(src, unit, dx, dy):
        there = ((unit[0] - dx) % SIDE, (unit[1] - dy) % SIDE, unit[2])
        slot = SLOT[there]
        copy = pltpu.make_async_remote_copy(
            src_ref=src,
            dst_ref=xbuf.at[pl.ds(slot * half_rows, half_rows)],
            send_sem=send_sem.at[len(sends)],
            recv_sem=recv_sem.at[slot],
            device_id=at(dx % SIDE, dy % SIDE),
            device_id_type=MESH,
        )
        copy.start()
        sends.append(unit)

    def piece(unit):
        return xbuf.at[pl.ds(SLOT[unit] * half_rows, half_rows)]

    def arrive(units):
        for unit in units:
            pltpu.make_async_remote_copy(
                src_ref=piece(unit), dst_ref=piece(unit), send_sem=send_sem.at[0],
                recv_sem=recv_sem.at[SLOT[unit]], device_id=at(1, 0), device_id_type=MESH,
            ).wait_recv()
            for dx, dy in onward(unit):
                send(piece(unit), unit, dx, dy)

    mine = [hidden_ref.at[pl.ds(h * half_rows, half_rows)] for h in (0, 1)]
    for d in (1, -1):
        send(mine[0], UNITS[0], d, 0)
        send(mine[1], UNITS[1], 0, d)
    for d in (1, -1):
        send(mine[0], UNITS[0], 0, d)
        send(mine[1], UNITS[1], d, 0)
    for d in (1, 2, 3):
        pl.semaphore_signal(entered, inc=1, device_id=at(0, d), device_id_type=MESH)

    lane = lax.broadcasted_iota(jnp.int32, (8, 128), 1)
    sub = lax.broadcasted_iota(jnp.int32, (8, 128), 0)

    def window(rows, start):
        a, o = divmod(start, 128)
        part = rows[a]
        if o:
            part = pltpu.roll(part, 128 - o, 1)
            if o + half_rows > 128:
                part = jnp.where(lane < 128 - o, part, pltpu.roll(rows[a + 1], 128 - o, 1))
        return part

    def source(unit):
        dx, dy, _ = unit
        return lax.rem(y + dy, SIDE) * SIDE + lax.rem(x + dx, SIDE)

    ids = [jnp.broadcast_to(target_ref[i : i + 1, :], (8, 128)) for i in range(count // 128)]
    for i in range(2 * PEERS):
        tok[i] = window(ids, i * half_rows)
    base = me * width
    for w in range(count // 128):
        label = jnp.zeros((8, 128), jnp.int32)
        for i in range(128 * w // half_rows, (128 * w + 127) // half_rows + 1):
            start = half_rows * i - 128 * w
            part = tok[source(UNITS[i]) * 2 + UNITS[i][2]]
            if start % 128:
                part = pltpu.roll(part, start % 128, 1)
            label = part if start <= 0 else jnp.where(lane < start, label, part)
        label = label - base
        label = jnp.where((label >= 0) & (label < width), label, -(1 << 24)) - sub
        lab[w // 2, :, (w % 2) * 128 : (w % 2 + 1) * 128] = label
    peak_ref[...] = jnp.full_like(peak_ref, LOW)
    sum_ref[...] = jnp.zeros_like(sum_ref)
    pick_ref[...] = jnp.zeros_like(pick_ref)
    spare = wbuf.shape[0] - width
    wbuf[width:, :] = jnp.zeros((spare, depth), jnp.bfloat16)
    low_row = lax.broadcasted_iota(jnp.int32, (32, 128), 0) >= 32 - spare
    low_lane = lax.broadcasted_iota(jnp.int32, (32, 128), 1) == 0
    low[...] = jnp.where(low_row & low_lane, LOW, 0.0).astype(jnp.bfloat16)

    own_copy.wait()
    needed = [-(-TILE * (t + 1) // half_rows) for t in range(tiles)]
    arrive(UNITS[2 : needed[0]])

    def multiply(*accs):
        acc = [[accs[0], accs[1]], [accs[2], accs[3]]]
        last = depth // TILE
        left = TILE - (depth - last * TILE)
        ones = (lax.broadcasted_iota(jnp.int32, (TILE, left), 1) == 0).astype(jnp.float32)
        ones = ones.astype(jnp.bfloat16)

        def push(k, t, reg):
            tokens = pl.ds(mult(t * TILE, TILE), TILE)
            if k < last:
                held = xbuf[tokens, k * TILE : (k + 1) * TILE]
            else:
                held = jnp.concatenate([xbuf[tokens, k * TILE :], ones], axis=1)
            for u in range(2):
                pltpu.matmul_push_rhs(held, reg, u, transpose=True)

        def where_is(n):
            t = n // per_tile if isinstance(n, int) else lax.div(n, per_tile)
            return t, n - t * per_tile

        def mm(t, s, after, slot):
            for k in range(last + 1):
                if k < last:
                    push(k + 1, t, (k + 1) % 2)
                else:
                    push(0, after, (k + 1) % 2)
                for u in range(2):
                    rows = pl.ds(mult(s * both + u * CHUNK, 16), CHUNK)
                    if k < last:
                        lhs = wbuf[rows, k * TILE : (k + 1) * TILE]
                    else:
                        pad = jnp.zeros((CHUNK, left), jnp.bfloat16)
                        if u == 1:
                            end = s // (per_tile - 1) if isinstance(s, int) else lax.div(s, per_tile - 1)
                            pad = jnp.concatenate([pad[16:], low[pl.ds(mult(end * 16, 16), 16), :]], axis=0)
                        lhs = jnp.concatenate([wbuf[rows, k * TILE :], pad], axis=1)
                    pltpu.matmul_acc_lhs(acc[u][slot], lhs, load_staged_rhs=k % 2)

        def statistics(t, s, slot):
            picked = pick_ref[t]
            for u in range(2):
                logits = pltpu.matmul_pop(acc[u][slot])
                label = lab[t] - (s * both + u * CHUNK)
                peak, total = peak_ref[t, u], sum_ref[t, u]
                for g in range(0, CHUNK // 8, GROUP):
                    part = [logits[j * 8 : (j + 1) * 8, :] for j in range(g, g + GROUP)]
                    top = part[0]
                    for v in part[1:]:
                        top = jnp.maximum(top, v)
                    old, peak = peak, jnp.maximum(peak, top)
                    terms = [jnp.exp(v - peak) for v in part]
                    while len(terms) > 1:
                        pairs = [a + b for a, b in zip(terms[::2], terms[1::2])]
                        terms = pairs + terms[2 * len(pairs) :]
                    total = total * jnp.exp(old - peak) + terms[0]
                    for i, v in enumerate(part):
                        picked = jnp.where(label == (g + i) * 8, v, picked)
                peak_ref[t, u], sum_ref[t, u] = peak, total
            pick_ref[t] = picked

        head_chunk(0).wait()
        push(0, 0, 0)
        mm(0, 0, 0, 0)

        @pl.loop(0, (steps - 2) // 2)
        def _(q):
            @pl.when(q < (per_tile - 3) // 2)
            def _():
                head_chunk(2 * q + 1).wait()
                head_chunk(2 * q + 2).wait()

            @pl.when(q == (per_tile - 3) // 2)
            def _():
                head_chunk(per_tile - 2).wait()
                head_chunk(per_tile - 1, last_rows).wait()

            for t in range(1, tiles):

                @pl.when(q == (t * per_tile - 2) // 2)
                def _():
                    arrive(UNITS[needed[t - 1] : needed[t]])

            spots = [where_is(2 * q + j) for j in range(4)]
            for j in range(2):
                mm(*spots[j + 1], spots[j + 2][0], (j + 1) % 2)
                statistics(*spots[j], j % 2)

        before, final = where_is(steps - 2), where_is(steps - 1)
        mm(*final, 0, 1)
        statistics(*before, 0)
        for u in range(2):
            pltpu.matmul_acc_lhs(acc[u][0], jnp.zeros((CHUNK, TILE), jnp.bfloat16), load_staged_rhs=0)
        statistics(*final, 1)
        for u in range(2):
            pltpu.matmul_pop(acc[u][0])

    pl.run_scoped(multiply, *[pltpu.ACC(u)((CHUNK, TILE), jnp.float32) for u in (0, 0, 1, 1)])

    sub_wide = lax.broadcasted_iota(jnp.int32, (8, TILE), 0)
    stats = []
    for t in range(tiles):
        peaks = jnp.concatenate([peak_ref[t, 0], peak_ref[t, 1]], axis=0)
        sums = jnp.concatenate([sum_ref[t, 0], sum_ref[t, 1]], axis=0)
        peak = jnp.max(peaks, axis=0, keepdims=True)
        total = jnp.sum(sums * jnp.exp(peaks - peak), axis=0, keepdims=True)
        picked = jnp.sum(pick_ref[t], axis=0, keepdims=True)
        packed = jnp.where(sub_wide == 0, peak, jnp.where(sub_wide == 1, total, picked))
        stats += [packed[:, i : i + 128] for i in range(0, TILE, 128)]
    for i, unit in enumerate(UNITS):
        flat[unit[2], source(unit)] = window(stats, i * half_rows)
    seq_count = owner_ref.shape[1]
    length = count // seq_count
    owned = seq_count // PEERS
    group = lane // length
    messages = [jnp.zeros((8, 128), jnp.float32) for _ in range(PEERS)]
    for v in range(PEERS):
        merged = jnp.where(lane < half_rows, flat[0, v], pltpu.roll(flat[1, v], half_rows, 1))
        turned = [merged] + [pltpu.roll(merged, i * length, 1) for i in range(1, 128 // length)]
        for j in range(owned):
            row = turned[-j % len(turned)]
            for i in range(1, owned):
                row = jnp.where(group < i, row, turned[(i - j) % len(turned)])
            seq = v * owned + j
            slot = jnp.broadcast_to(owner_ref[:, seq : seq + 1], (8, 128)) - group
            for to in range(PEERS):
                messages[to] = jnp.where(slot == to * owned, row, messages[to])
    for to in range(PEERS):
        ordered[to] = messages[to]

    pl.semaphore_wait(entered, 3)
    outs = []
    for d in range(1, PEERS):
        to = lax.rem(me + d, PEERS)
        copy = pltpu.make_async_remote_copy(
            src_ref=ordered.at[to],
            dst_ref=got.at[d],
            send_sem=out_sem.at[d],
            recv_sem=in_sem.at[d],
            device_id={"vocab": to},
            device_id_type=MESH,
        )
        copy.start()
        outs.append(copy)
    got[0] = ordered[me]
    for copy in outs:
        copy.wait_recv()
    parts = [got[d] for d in range(PEERS)]
    top = parts[0]
    for part in parts[1:]:
        top = jnp.maximum(top, part)
    total, picked = jnp.zeros_like(top), jnp.zeros_like(top)
    for part in parts:
        total = total + part * pltpu.roll(jnp.exp(part - top), 1, 0)
        picked = picked + part
    loss = top[0:1, :] + jnp.log(total[1:2, :]) - picked[2:3, :]
    for i in range(owned):
        out_ref[i : i + 1, :] = loss[:, i * length : (i + 1) * length]
    for i, unit in enumerate(sends):
        pltpu.make_async_remote_copy(
            src_ref=piece(unit), dst_ref=piece(unit), send_sem=send_sem.at[i], recv_sem=recv_sem.at[0],
            device_id=at(1, 0), device_id_type=MESH,
        ).wait_send()
    for copy in outs:
        copy.wait_send()


def local(hidden, target_ids, owner, head):
    depth = hidden.shape[1]
    count = target_ids.shape[0]
    rows = head.shape[1]
    tall = -(-rows // (2 * CHUNK)) * 2 * CHUNK
    seq_count = owner.shape[1]
    tiles = count // TILE
    vmem = pl.BlockSpec(memory_space=pltpu.VMEM)
    anywhere = pl.BlockSpec(memory_space=pl.ANY)
    f32 = jnp.float32
    return pl.pallas_call(
        kernel,
        out_shape=jax.ShapeDtypeStruct((seq_count // PEERS, count // seq_count), f32),
        in_specs=[anywhere, vmem, vmem, anywhere],
        out_specs=vmem,
        scratch_shapes=[
            pltpu.VMEM((count, depth), jnp.bfloat16),
            pltpu.VMEM((tall, depth), jnp.bfloat16),
            pltpu.VMEM((32, 128), jnp.bfloat16),
            pltpu.VMEM((2 * PEERS, 8, 128), jnp.int32),
            pltpu.VMEM((tiles, 8, TILE), jnp.int32),
            pltpu.VMEM((tiles, 2, 8, TILE), f32),
            pltpu.VMEM((tiles, 2, 8, TILE), f32),
            pltpu.VMEM((tiles, 8, TILE), f32),
            pltpu.VMEM((2, PEERS, 8, 128), f32),
            pltpu.VMEM((PEERS, 8, 128), f32),
            pltpu.VMEM((PEERS, 8, 128), f32),
            pltpu.SemaphoreType.DMA,
            pltpu.SemaphoreType.DMA((tall // (2 * CHUNK),)),
            pltpu.SemaphoreType.DMA((len(UNITS),)),
            pltpu.SemaphoreType.DMA((len(UNITS),)),
            pltpu.SemaphoreType.DMA((PEERS,)),
            pltpu.SemaphoreType.DMA((PEERS,)),
            pltpu.SemaphoreType.REGULAR,
        ],
        compiler_params=pltpu.CompilerParams(
            collective_id=0,
            has_side_effects=True,
        ),
    )(hidden, target_ids.reshape(count // 128, 128), owner, head.T)


def solution(mesh):
    return jax.shard_map(
        local,
        mesh=mesh,
        in_specs=(P(("dp", "vocab"), None), P("dp"), P("dp", None), P(None, "vocab")),
        out_specs=P(("dp", "vocab"), None),
        check_vma=False,
    )
```

```python
import jax
import jax.numpy as jnp
from jax import lax
from jax.experimental import pallas as pl
from jax.experimental.pallas import tpu as pltpu
from jax.sharding import PartitionSpec as P

MESH = pl.DeviceIdType.MESH
SIDE = 4
PEERS = SIDE * SIDE
TILE = 256
CHUNK = 432
GROUP = 9
LOW = -1e30

OWN = [(0, 0, 0), (0, 0, 1)]
FIRST = [(1, 0, 0), (3, 0, 0), (0, 1, 1), (0, 3, 1)]
SECOND = [(2, 0, 0), (0, 2, 1)]
DIRECT = [(0, 1, 0), (0, 3, 0), (1, 0, 1), (3, 0, 1), (0, 2, 0), (2, 0, 1)]
RELAYED = [
    (dx, dy, half)
    for a, b in ((1, 1), (1, 3), (3, 1), (3, 3), (1, 2), (3, 2), (2, 1), (2, 3), (2, 2))
    for dx, dy, half in ((a, b, 0), (b, a, 1))
]
UNITS = OWN + FIRST + SECOND + DIRECT + RELAYED
SLOT = {unit: i for i, unit in enumerate(UNITS)}


def mult(value, of):
    return value if isinstance(value, int) else pl.multiple_of(value, of)


def kernel(
    hidden_ref, target_ref, owner_ref, head_ref, out_ref,
    xbuf, wbuf, low, tok, lab, peak_ref, sum_ref, pick_ref, flat, ordered, got,
    own_sem, head_sem, send_sem, recv_sem, out_sem, in_sem, entered,
):
    rows_own, depth = hidden_ref.shape
    width = head_ref.shape[0]
    half_rows = rows_own // 2
    count = xbuf.shape[0]
    tiles = count // TILE
    both = 2 * CHUNK
    per_tile = wbuf.shape[0] // both
    steps = tiles * per_tile
    last_rows = width - (per_tile - 1) * both

    me = lax.axis_index("vocab")
    y, x = lax.div(me, SIDE), lax.rem(me, SIDE)

    def at(dx, dy):
        return {"vocab": lax.rem(y + dy, SIDE) * SIDE + lax.rem(x + dx, SIDE)}

    own_copy = pltpu.make_async_copy(hidden_ref, xbuf.at[pl.ds(0, rows_own)], own_sem)
    own_copy.start()

    def head_chunk(i, rows=both):
        part = pl.ds(mult(i * both, 16), rows)
        return pltpu.make_async_copy(head_ref.at[part], wbuf.at[part], head_sem.at[i])

    for i in range(per_tile - 1):
        head_chunk(i).start()
    head_chunk(per_tile - 1, last_rows).start()

    barrier = pltpu.get_barrier_semaphore()
    for d in (1, 2, 3):
        pl.semaphore_signal(barrier, inc=1, device_id=at(d, 0), device_id_type=MESH)
        pl.semaphore_signal(barrier, inc=1, device_id=at(0, d), device_id_type=MESH)
    pl.semaphore_wait(barrier, 6)

    sends = []

    def send(src, unit, dx, dy):
        there = ((unit[0] - dx) % SIDE, (unit[1] - dy) % SIDE, unit[2])
        slot = SLOT[there]
        copy = pltpu.make_async_remote_copy(
            src_ref=src,
            dst_ref=xbuf.at[pl.ds(slot * half_rows, half_rows)],
            send_sem=send_sem.at[len(sends)],
            recv_sem=recv_sem.at[slot],
            device_id=at(dx, dy),
            device_id_type=MESH,
        )
        copy.start()
        sends.append(unit)

    def arrived(slot):
        here = xbuf.at[pl.ds(mult(slot * half_rows, half_rows), half_rows)]
        pltpu.make_async_remote_copy(
            src_ref=here, dst_ref=here, send_sem=send_sem.at[0], recv_sem=recv_sem.at[slot],
            device_id=at(1, 0), device_id_type=MESH,
        ).wait_recv()

    def piece(unit):
        return xbuf.at[pl.ds(SLOT[unit] * half_rows, half_rows)]

    mine = [hidden_ref.at[pl.ds(h * half_rows, half_rows)] for h in (0, 1)]
    for d in (1, 3, 2):
        send(mine[0], OWN[0], d, 0)
        send(mine[1], OWN[1], 0, d)
    for d in (1, 2, 3):
        pl.semaphore_signal(entered, inc=1, device_id=at(0, d), device_id_type=MESH)

    lane = lax.broadcasted_iota(jnp.int32, (8, 128), 1)
    sub = lax.broadcasted_iota(jnp.int32, (8, 128), 0)

    def window(rows, start):
        a, o = divmod(start, 128)
        part = rows[a]
        if o:
            part = pltpu.roll(part, 128 - o, 1)
            if o + half_rows > 128:
                part = jnp.where(lane < 128 - o, part, pltpu.roll(rows[a + 1], 128 - o, 1))
        return part

    def source(unit):
        dx, dy, _ = unit
        return lax.rem(y + dy, SIDE) * SIDE + lax.rem(x + dx, SIDE)

    ids = [jnp.broadcast_to(target_ref[i : i + 1, :], (8, 128)) for i in range(count // 128)]
    for i in range(2 * PEERS):
        tok[i] = window(ids, i * half_rows)
    base = me * width
    for w in range(count // 128):
        label = jnp.zeros((8, 128), jnp.int32)
        for i in range(128 * w // half_rows, (128 * w + 127) // half_rows + 1):
            start = half_rows * i - 128 * w
            part = tok[source(UNITS[i]) * 2 + UNITS[i][2]]
            if start % 128:
                part = pltpu.roll(part, start % 128, 1)
            label = part if start <= 0 else jnp.where(lane < start, label, part)
        label = label - base
        label = jnp.where((label >= 0) & (label < width), label, -(1 << 24)) - sub
        lab[w // 2, :, (w % 2) * 128 : (w % 2 + 1) * 128] = label
    peak_ref[...] = jnp.full_like(peak_ref, LOW)
    sum_ref[...] = jnp.zeros_like(sum_ref)
    pick_ref[...] = jnp.zeros_like(pick_ref)
    spare = wbuf.shape[0] - width
    wbuf[width:, :] = jnp.zeros((spare, depth), jnp.bfloat16)
    low_row = lax.broadcasted_iota(jnp.int32, (32, 128), 0) >= 32 - spare
    low_lane = lax.broadcasted_iota(jnp.int32, (32, 128), 1) == 0
    low[...] = jnp.where(low_row & low_lane, LOW, 0.0).astype(jnp.bfloat16)

    own_copy.wait()
    for unit in FIRST:
        arrived(SLOT[unit])
    for turn in ((1, 3), (2,)):
        for d in turn:
            send(mine[0], OWN[0], 0, d)
            send(mine[1], OWN[1], d, 0)
        for unit in FIRST:
            for d in turn:
                send(piece(unit), unit, *((0, d) if unit[2] == 0 else (d, 0)))

    def multiply(*accs):
        acc = [[accs[0], accs[1]], [accs[2], accs[3]]]
        last = depth // TILE
        left = TILE - (depth - last * TILE)
        ones = (lax.broadcasted_iota(jnp.int32, (TILE, left), 1) == 0).astype(jnp.float32)
        ones = ones.astype(jnp.bfloat16)

        def push(k, t, reg):
            tokens = pl.ds(mult(t * TILE, TILE), TILE)
            if k < last:
                held = xbuf[tokens, k * TILE : (k + 1) * TILE]
            else:
                held = jnp.concatenate([xbuf[tokens, k * TILE :], ones], axis=1)
            for u in range(2):
                pltpu.matmul_push_rhs(held, reg, u, transpose=True)

        def where_is(n):
            t = n // per_tile if isinstance(n, int) else lax.div(n, per_tile)
            return t, n - t * per_tile

        def mm(t, s, after, slot):
            for k in range(last + 1):
                if k < last:
                    push(k + 1, t, (k + 1) % 2)
                else:
                    push(0, after, (k + 1) % 2)
                for u in range(2):
                    rows = pl.ds(mult(s * both + u * CHUNK, 16), CHUNK)
                    if k < last:
                        lhs = wbuf[rows, k * TILE : (k + 1) * TILE]
                    else:
                        pad = jnp.zeros((CHUNK, left), jnp.bfloat16)
                        if u == 1:
                            end = s // (per_tile - 1) if isinstance(s, int) else lax.div(s, per_tile - 1)
                            pad = jnp.concatenate([pad[16:], low[pl.ds(mult(end * 16, 16), 16), :]], axis=0)
                        lhs = jnp.concatenate([wbuf[rows, k * TILE :], pad], axis=1)
                    pltpu.matmul_acc_lhs(acc[u][slot], lhs, load_staged_rhs=k % 2)

        def statistics(t, s, slot):
            picked = pick_ref[t]
            for u in range(2):
                logits = pltpu.matmul_pop(acc[u][slot])
                label = lab[t] - (s * both + u * CHUNK)
                peak, total = peak_ref[t, u], sum_ref[t, u]
                for g in range(0, CHUNK // 8, GROUP):
                    part = [logits[j * 8 : (j + 1) * 8, :] for j in range(g, g + GROUP)]
                    top = part[0]
                    for v in part[1:]:
                        top = jnp.maximum(top, v)
                    old, peak = peak, jnp.maximum(peak, top)
                    terms = [jnp.exp(v - peak) for v in part]
                    while len(terms) > 1:
                        pairs = [a + b for a, b in zip(terms[::2], terms[1::2])]
                        terms = pairs + terms[2 * len(pairs) :]
                    total = total * jnp.exp(old - peak) + terms[0]
                    for i, v in enumerate(part):
                        picked = jnp.where(label == (g + i) * 8, v, picked)
                peak_ref[t, u], sum_ref[t, u] = peak, total
            pick_ref[t] = picked

        head_chunk(0).wait()
        push(0, 0, 0)
        mm(0, 0, 0, 0)

        @pl.loop(0, (steps - 2) // 2)
        def _(q):
            @pl.when(q < (per_tile - 3) // 2)
            def _():
                head_chunk(2 * q + 1).wait()
                head_chunk(2 * q + 2).wait()

            @pl.when(q == (per_tile - 3) // 2)
            def _():
                head_chunk(per_tile - 2).wait()
                head_chunk(per_tile - 1, last_rows).wait()

            for t in range(1, tiles):

                @pl.when(q == (t * per_tile - 2) // 2)
                def _():
                    lo, hi = (-(-TILE * i // half_rows) for i in (t, t + 1))
                    if t == 1:
                        for unit in SECOND:
                            arrived(SLOT[unit])
                            for d in (1, 3, 2):
                                send(piece(unit), unit, *((0, d) if unit[2] == 0 else (d, 0)))
                        lo += len(SECOND)

                    @pl.loop(lo, hi)
                    def _(slot):
                        arrived(slot)

            spots = [where_is(2 * q + j) for j in range(4)]
            for j in range(2):
                mm(*spots[j + 1], spots[j + 2][0], (j + 1) % 2)
                statistics(*spots[j], j % 2)

        before, final = where_is(steps - 2), where_is(steps - 1)
        mm(*final, 0, 1)
        statistics(*before, 0)
        for u in range(2):
            pltpu.matmul_acc_lhs(acc[u][0], jnp.zeros((CHUNK, TILE), jnp.bfloat16), load_staged_rhs=0)
        statistics(*final, 1)
        for u in range(2):
            pltpu.matmul_pop(acc[u][0])

    pl.run_scoped(multiply, *[pltpu.ACC(u)((CHUNK, TILE), jnp.float32) for u in (0, 0, 1, 1)])

    sub_wide = lax.broadcasted_iota(jnp.int32, (8, TILE), 0)
    stats = []
    for t in range(tiles):
        peaks = jnp.concatenate([peak_ref[t, 0], peak_ref[t, 1]], axis=0)
        sums = jnp.concatenate([sum_ref[t, 0], sum_ref[t, 1]], axis=0)
        peak = jnp.max(peaks, axis=0, keepdims=True)
        total = jnp.sum(sums * jnp.exp(peaks - peak), axis=0, keepdims=True)
        picked = jnp.sum(pick_ref[t], axis=0, keepdims=True)
        packed = jnp.where(sub_wide == 0, peak, jnp.where(sub_wide == 1, total, picked))
        stats += [packed[:, i : i + 128] for i in range(0, TILE, 128)]
    for i, unit in enumerate(UNITS):
        flat[unit[2], source(unit)] = window(stats, i * half_rows)
    seq_count = owner_ref.shape[1]
    length = count // seq_count
    owned = seq_count // PEERS
    group = lane // length
    messages = [jnp.zeros((8, 128), jnp.float32) for _ in range(PEERS)]
    for v in range(PEERS):
        merged = jnp.where(lane < half_rows, flat[0, v], pltpu.roll(flat[1, v], half_rows, 1))
        turned = [merged] + [pltpu.roll(merged, i * length, 1) for i in range(1, 128 // length)]
        for j in range(owned):
            row = turned[-j % len(turned)]
            for i in range(1, owned):
                row = jnp.where(group < i, row, turned[(i - j) % len(turned)])
            seq = v * owned + j
            slot = jnp.broadcast_to(owner_ref[:, seq : seq + 1], (8, 128)) - group
            for to in range(PEERS):
                messages[to] = jnp.where(slot == to * owned, row, messages[to])
    for to in range(PEERS):
        ordered[to] = messages[to]

    pl.semaphore_wait(entered, 3)
    outs = []
    for d in range(1, PEERS):
        to = lax.rem(me + d, PEERS)
        copy = pltpu.make_async_remote_copy(
            src_ref=ordered.at[to],
            dst_ref=got.at[d],
            send_sem=out_sem.at[d],
            recv_sem=in_sem.at[d],
            device_id={"vocab": to},
            device_id_type=MESH,
        )
        copy.start()
        outs.append(copy)
    got[0] = ordered[me]
    for copy in outs:
        copy.wait_recv()
    parts = [got[d] for d in range(PEERS)]
    top = parts[0]
    for part in parts[1:]:
        top = jnp.maximum(top, part)
    total, picked = jnp.zeros_like(top), jnp.zeros_like(top)
    for part in parts:
        total = total + part * pltpu.roll(jnp.exp(part - top), 1, 0)
        picked = picked + part
    loss = top[0:1, :] + jnp.log(total[1:2, :]) - picked[2:3, :]
    for i in range(owned):
        out_ref[i : i + 1, :] = loss[:, i * length : (i + 1) * length]
    for i, unit in enumerate(sends):
        pltpu.make_async_remote_copy(
            src_ref=piece(unit), dst_ref=piece(unit), send_sem=send_sem.at[i], recv_sem=recv_sem.at[0],
            device_id=at(1, 0), device_id_type=MESH,
        ).wait_send()
    for copy in outs:
        copy.wait_send()


def local(hidden, target_ids, owner, head):
    depth = hidden.shape[1]
    count = target_ids.shape[0]
    rows = head.shape[1]
    tall = -(-rows // (2 * CHUNK)) * 2 * CHUNK
    seq_count = owner.shape[1]
    tiles = count // TILE
    vmem = pl.BlockSpec(memory_space=pltpu.VMEM)
    anywhere = pl.BlockSpec(memory_space=pl.ANY)
    f32 = jnp.float32
    return pl.pallas_call(
        kernel,
        out_shape=jax.ShapeDtypeStruct((seq_count // PEERS, count // seq_count), f32),
        in_specs=[anywhere, vmem, vmem, anywhere],
        out_specs=vmem,
        scratch_shapes=[
            pltpu.VMEM((count, depth), jnp.bfloat16),
            pltpu.VMEM((tall, depth), jnp.bfloat16),
            pltpu.VMEM((32, 128), jnp.bfloat16),
            pltpu.VMEM((2 * PEERS, 8, 128), jnp.int32),
            pltpu.VMEM((tiles, 8, TILE), jnp.int32),
            pltpu.VMEM((tiles, 2, 8, TILE), f32),
            pltpu.VMEM((tiles, 2, 8, TILE), f32),
            pltpu.VMEM((tiles, 8, TILE), f32),
            pltpu.VMEM((2, PEERS, 8, 128), f32),
            pltpu.VMEM((PEERS, 8, 128), f32),
            pltpu.VMEM((PEERS, 8, 128), f32),
            pltpu.SemaphoreType.DMA,
            pltpu.SemaphoreType.DMA((tall // (2 * CHUNK),)),
            pltpu.SemaphoreType.DMA((len(UNITS),)),
            pltpu.SemaphoreType.DMA((len(UNITS),)),
            pltpu.SemaphoreType.DMA((PEERS,)),
            pltpu.SemaphoreType.DMA((PEERS,)),
            pltpu.SemaphoreType.REGULAR,
        ],
        compiler_params=pltpu.CompilerParams(
            collective_id=0,
            has_side_effects=True,
        ),
    )(hidden, target_ids.reshape(count // 128, 128), owner, head.T)


def solution(mesh):
    return jax.shard_map(
        local,
        mesh=mesh,
        in_specs=(P(("dp", "vocab"), None), P("dp"), P("dp", None), P(None, "vocab")),
        out_specs=P(("dp", "vocab"), None),
        check_vma=False,
    )
```

```python
import jax
import jax.numpy as jnp
from jax import lax
from jax.experimental import pallas as pl
from jax.experimental.pallas import tpu as pltpu
from jax.sharding import PartitionSpec as P

MESH = pl.DeviceIdType.MESH
SIDE = 4
PEERS = SIDE * SIDE
TILE = 256
CHUNK = 432
GROUP = 9
LOW = -1e30

OWN = [(0, 0, 0), (0, 0, 1)]
FIRST = [(1, 0, 0), (3, 0, 0), (0, 1, 1), (0, 3, 1)]
SECOND = [(2, 0, 0), (0, 2, 1)]
DIRECT = [(0, 1, 0), (0, 3, 0), (1, 0, 1), (3, 0, 1), (0, 2, 0), (2, 0, 1)]
RELAYED = [
    (dx, dy, half)
    for a, b in ((1, 1), (1, 3), (3, 1), (3, 3), (1, 2), (3, 2), (2, 1), (2, 3), (2, 2))
    for dx, dy, half in ((a, b, 0), (b, a, 1))
]
UNITS = OWN + FIRST + SECOND + DIRECT + RELAYED
SLOT = {unit: i for i, unit in enumerate(UNITS)}


def mult(value, of):
    return value if isinstance(value, int) else pl.multiple_of(value, of)


def kernel(
    hidden_ref, target_ref, owner_ref, head_ref, out_ref,
    xbuf, wbuf, low, tok, lab, peak_ref, sum_ref, pick_ref, flat, ordered, got,
    own_sem, head_sem, send_sem, recv_sem, out_sem, in_sem, entered,
):
    rows_own, depth = hidden_ref.shape
    width = head_ref.shape[0]
    half_rows = rows_own // 2
    count = xbuf.shape[0]
    tiles = count // TILE
    both = 2 * CHUNK
    per_tile = wbuf.shape[0] // both
    steps = tiles * per_tile
    last_rows = width - (per_tile - 1) * both

    me = lax.axis_index("vocab")
    y, x = lax.div(me, SIDE), lax.rem(me, SIDE)

    def at(dx, dy):
        return {"vocab": lax.rem(y + dy, SIDE) * SIDE + lax.rem(x + dx, SIDE)}

    own_copy = pltpu.make_async_copy(hidden_ref, xbuf.at[pl.ds(0, rows_own)], own_sem)
    own_copy.start()

    def head_chunk(i, rows=both):
        part = pl.ds(mult(i * both, 16), rows)
        return pltpu.make_async_copy(head_ref.at[part], wbuf.at[part], head_sem.at[i])

    for i in range(per_tile - 1):
        head_chunk(i).start()
    head_chunk(per_tile - 1, last_rows).start()

    barrier = pltpu.get_barrier_semaphore()
    for d in (1, 2, 3):
        pl.semaphore_signal(barrier, inc=1, device_id=at(d, 0), device_id_type=MESH)
        pl.semaphore_signal(barrier, inc=1, device_id=at(0, d), device_id_type=MESH)
    pl.semaphore_wait(barrier, 6)

    sends = []

    def send(src, unit, dx, dy):
        there = ((unit[0] - dx) % SIDE, (unit[1] - dy) % SIDE, unit[2])
        slot = SLOT[there]
        copy = pltpu.make_async_remote_copy(
            src_ref=src,
            dst_ref=xbuf.at[pl.ds(slot * half_rows, half_rows)],
            send_sem=send_sem.at[len(sends)],
            recv_sem=recv_sem.at[slot],
            device_id=at(dx, dy),
            device_id_type=MESH,
        )
        copy.start()
        sends.append(unit)

    def arrived(slot):
        here = xbuf.at[pl.ds(mult(slot * half_rows, half_rows), half_rows)]
        pltpu.make_async_remote_copy(
            src_ref=here, dst_ref=here, send_sem=send_sem.at[0], recv_sem=recv_sem.at[slot],
            device_id=at(1, 0), device_id_type=MESH,
        ).wait_recv()

    def piece(unit):
        return xbuf.at[pl.ds(SLOT[unit] * half_rows, half_rows)]

    mine = [hidden_ref.at[pl.ds(h * half_rows, half_rows)] for h in (0, 1)]
    for d in (1, 3, 2):
        send(mine[0], OWN[0], d, 0)
        send(mine[1], OWN[1], 0, d)
    for d in (1, 2, 3):
        pl.semaphore_signal(entered, inc=1, device_id=at(0, d), device_id_type=MESH)

    lane = lax.broadcasted_iota(jnp.int32, (8, 128), 1)
    sub = lax.broadcasted_iota(jnp.int32, (8, 128), 0)

    def window(rows, start):
        a, o = divmod(start, 128)
        part = rows[a]
        if o:
            part = pltpu.roll(part, 128 - o, 1)
            if o + half_rows > 128:
                part = jnp.where(lane < 128 - o, part, pltpu.roll(rows[a + 1], 128 - o, 1))
        return part

    def source(unit):
        dx, dy, _ = unit
        return lax.rem(y + dy, SIDE) * SIDE + lax.rem(x + dx, SIDE)

    ids = [jnp.broadcast_to(target_ref[i : i + 1, :], (8, 128)) for i in range(count // 128)]
    for i in range(2 * PEERS):
        tok[i] = window(ids, i * half_rows)
    base = me * width
    for w in range(count // 128):
        label = jnp.zeros((8, 128), jnp.int32)
        for i in range(128 * w // half_rows, (128 * w + 127) // half_rows + 1):
            start = half_rows * i - 128 * w
            part = tok[source(UNITS[i]) * 2 + UNITS[i][2]]
            if start % 128:
                part = pltpu.roll(part, start % 128, 1)
            label = part if start <= 0 else jnp.where(lane < start, label, part)
        label = label - base
        label = jnp.where((label >= 0) & (label < width), label, -(1 << 24)) - sub
        lab[w // 2, :, (w % 2) * 128 : (w % 2 + 1) * 128] = label
    peak_ref[...] = jnp.full_like(peak_ref, LOW)
    sum_ref[...] = jnp.zeros_like(sum_ref)
    pick_ref[...] = jnp.zeros_like(pick_ref)
    spare = wbuf.shape[0] - width
    wbuf[width:, :] = jnp.zeros((spare, depth), jnp.bfloat16)
    low_row = lax.broadcasted_iota(jnp.int32, (32, 128), 0) >= 32 - spare
    low_lane = lax.broadcasted_iota(jnp.int32, (32, 128), 1) == 0
    low[...] = jnp.where(low_row & low_lane, LOW, 0.0).astype(jnp.bfloat16)

    own_copy.wait()
    for unit in FIRST:
        arrived(SLOT[unit])
    def spread(turn):
        for d in turn:
            send(mine[0], OWN[0], 0, d)
            send(mine[1], OWN[1], d, 0)
        for unit in FIRST:
            for d in turn:
                send(piece(unit), unit, *((0, d) if unit[2] == 0 else (d, 0)))

    spread((1, 3))

    def multiply(*accs):
        acc = [[accs[0], accs[1]], [accs[2], accs[3]]]
        last = depth // TILE
        left = TILE - (depth - last * TILE)
        ones = (lax.broadcasted_iota(jnp.int32, (TILE, left), 1) == 0).astype(jnp.float32)
        ones = ones.astype(jnp.bfloat16)

        def push(k, t, reg):
            tokens = pl.ds(mult(t * TILE, TILE), TILE)
            if k < last:
                held = xbuf[tokens, k * TILE : (k + 1) * TILE]
            else:
                held = jnp.concatenate([xbuf[tokens, k * TILE :], ones], axis=1)
            for u in range(2):
                pltpu.matmul_push_rhs(held, reg, u, transpose=True)

        def where_is(n):
            t = n // per_tile if isinstance(n, int) else lax.div(n, per_tile)
            return t, n - t * per_tile

        def mm(t, s, after, slot):
            for k in range(last + 1):
                if k < last:
                    push(k + 1, t, (k + 1) % 2)
                else:
                    push(0, after, (k + 1) % 2)
                for u in range(2):
                    rows = pl.ds(mult(s * both + u * CHUNK, 16), CHUNK)
                    if k < last:
                        lhs = wbuf[rows, k * TILE : (k + 1) * TILE]
                    else:
                        pad = jnp.zeros((CHUNK, left), jnp.bfloat16)
                        if u == 1:
                            end = s // (per_tile - 1) if isinstance(s, int) else lax.div(s, per_tile - 1)
                            pad = jnp.concatenate([pad[16:], low[pl.ds(mult(end * 16, 16), 16), :]], axis=0)
                        lhs = jnp.concatenate([wbuf[rows, k * TILE :], pad], axis=1)
                    pltpu.matmul_acc_lhs(acc[u][slot], lhs, load_staged_rhs=k % 2)

        def statistics(t, s, slot):
            picked = pick_ref[t]
            for u in range(2):
                logits = pltpu.matmul_pop(acc[u][slot])
                label = lab[t] - (s * both + u * CHUNK)
                peak, total = peak_ref[t, u], sum_ref[t, u]
                for g in range(0, CHUNK // 8, GROUP):
                    part = [logits[j * 8 : (j + 1) * 8, :] for j in range(g, g + GROUP)]
                    top = part[0]
                    for v in part[1:]:
                        top = jnp.maximum(top, v)
                    old, peak = peak, jnp.maximum(peak, top)
                    terms = [jnp.exp(v - peak) for v in part]
                    while len(terms) > 1:
                        pairs = [a + b for a, b in zip(terms[::2], terms[1::2])]
                        terms = pairs + terms[2 * len(pairs) :]
                    total = total * jnp.exp(old - peak) + terms[0]
                    for i, v in enumerate(part):
                        picked = jnp.where(label == (g + i) * 8, v, picked)
                peak_ref[t, u], sum_ref[t, u] = peak, total
            pick_ref[t] = picked

        head_chunk(0).wait()
        push(0, 0, 0)
        mm(0, 0, 0, 0)

        @pl.loop(0, (steps - 2) // 2)
        def _(q):
            @pl.when(q < (per_tile - 3) // 2)
            def _():
                head_chunk(2 * q + 1).wait()
                head_chunk(2 * q + 2).wait()

            @pl.when(q == (per_tile - 3) // 2)
            def _():
                head_chunk(per_tile - 2).wait()
                head_chunk(per_tile - 1, last_rows).wait()

            @pl.when(q == 2)
            def _():
                spread((2,))

            for t in range(1, tiles):

                @pl.when(q == (t * per_tile - 2) // 2)
                def _():
                    lo, hi = (-(-TILE * i // half_rows) for i in (t, t + 1))
                    if t == 1:
                        for unit in SECOND:
                            arrived(SLOT[unit])
                            for d in (1, 3, 2):
                                send(piece(unit), unit, *((0, d) if unit[2] == 0 else (d, 0)))
                        lo += len(SECOND)

                    @pl.loop(lo, hi)
                    def _(slot):
                        arrived(slot)

            spots = [where_is(2 * q + j) for j in range(4)]
            for j in range(2):
                mm(*spots[j + 1], spots[j + 2][0], (j + 1) % 2)
                statistics(*spots[j], j % 2)

        before, final = where_is(steps - 2), where_is(steps - 1)
        mm(*final, 0, 1)
        statistics(*before, 0)
        for u in range(2):
            pltpu.matmul_acc_lhs(acc[u][0], jnp.zeros((CHUNK, TILE), jnp.bfloat16), load_staged_rhs=0)
        statistics(*final, 1)
        for u in range(2):
            pltpu.matmul_pop(acc[u][0])

    pl.run_scoped(multiply, *[pltpu.ACC(u)((CHUNK, TILE), jnp.float32) for u in (0, 0, 1, 1)])

    sub_wide = lax.broadcasted_iota(jnp.int32, (8, TILE), 0)
    stats = []
    for t in range(tiles):
        peaks = jnp.concatenate([peak_ref[t, 0], peak_ref[t, 1]], axis=0)
        sums = jnp.concatenate([sum_ref[t, 0], sum_ref[t, 1]], axis=0)
        peak = jnp.max(peaks, axis=0, keepdims=True)
        total = jnp.sum(sums * jnp.exp(peaks - peak), axis=0, keepdims=True)
        picked = jnp.sum(pick_ref[t], axis=0, keepdims=True)
        packed = jnp.where(sub_wide == 0, peak, jnp.where(sub_wide == 1, total, picked))
        stats += [packed[:, i : i + 128] for i in range(0, TILE, 128)]
    for i, unit in enumerate(UNITS):
        flat[unit[2], source(unit)] = window(stats, i * half_rows)
    seq_count = owner_ref.shape[1]
    length = count // seq_count
    owned = seq_count // PEERS
    group = lane // length
    messages = [jnp.zeros((8, 128), jnp.float32) for _ in range(PEERS)]
    for v in range(PEERS):
        merged = jnp.where(lane < half_rows, flat[0, v], pltpu.roll(flat[1, v], half_rows, 1))
        turned = [merged] + [pltpu.roll(merged, i * length, 1) for i in range(1, 128 // length)]
        for j in range(owned):
            row = turned[-j % len(turned)]
            for i in range(1, owned):
                row = jnp.where(group < i, row, turned[(i - j) % len(turned)])
            seq = v * owned + j
            slot = jnp.broadcast_to(owner_ref[:, seq : seq + 1], (8, 128)) - group
            for to in range(PEERS):
                messages[to] = jnp.where(slot == to * owned, row, messages[to])
    for to in range(PEERS):
        ordered[to] = messages[to]

    pl.semaphore_wait(entered, 3)
    outs = []
    for d in range(1, PEERS):
        to = lax.rem(me + d, PEERS)
        copy = pltpu.make_async_remote_copy(
            src_ref=ordered.at[to],
            dst_ref=got.at[d],
            send_sem=out_sem.at[d],
            recv_sem=in_sem.at[d],
            device_id={"vocab": to},
            device_id_type=MESH,
        )
        copy.start()
        outs.append(copy)
    got[0] = ordered[me]
    for copy in outs:
        copy.wait_recv()
    parts = [got[d] for d in range(PEERS)]
    top = parts[0]
    for part in parts[1:]:
        top = jnp.maximum(top, part)
    total, picked = jnp.zeros_like(top), jnp.zeros_like(top)
    for part in parts:
        total = total + part * pltpu.roll(jnp.exp(part - top), 1, 0)
        picked = picked + part
    loss = top[0:1, :] + jnp.log(total[1:2, :]) - picked[2:3, :]
    for i in range(owned):
        out_ref[i : i + 1, :] = loss[:, i * length : (i + 1) * length]
    for i, unit in enumerate(sends):
        pltpu.make_async_remote_copy(
            src_ref=piece(unit), dst_ref=piece(unit), send_sem=send_sem.at[i], recv_sem=recv_sem.at[0],
            device_id=at(1, 0), device_id_type=MESH,
        ).wait_send()
    for copy in outs:
        copy.wait_send()


def local(hidden, target_ids, owner, head):
    depth = hidden.shape[1]
    count = target_ids.shape[0]
    rows = head.shape[1]
    tall = -(-rows // (2 * CHUNK)) * 2 * CHUNK
    seq_count = owner.shape[1]
    tiles = count // TILE
    vmem = pl.BlockSpec(memory_space=pltpu.VMEM)
    anywhere = pl.BlockSpec(memory_space=pl.ANY)
    f32 = jnp.float32
    return pl.pallas_call(
        kernel,
        out_shape=jax.ShapeDtypeStruct((seq_count // PEERS, count // seq_count), f32),
        in_specs=[anywhere, vmem, vmem, anywhere],
        out_specs=vmem,
        scratch_shapes=[
            pltpu.VMEM((count, depth), jnp.bfloat16),
            pltpu.VMEM((tall, depth), jnp.bfloat16),
            pltpu.VMEM((32, 128), jnp.bfloat16),
            pltpu.VMEM((2 * PEERS, 8, 128), jnp.int32),
            pltpu.VMEM((tiles, 8, TILE), jnp.int32),
            pltpu.VMEM((tiles, 2, 8, TILE), f32),
            pltpu.VMEM((tiles, 2, 8, TILE), f32),
            pltpu.VMEM((tiles, 8, TILE), f32),
            pltpu.VMEM((2, PEERS, 8, 128), f32),
            pltpu.VMEM((PEERS, 8, 128), f32),
            pltpu.VMEM((PEERS, 8, 128), f32),
            pltpu.SemaphoreType.DMA,
            pltpu.SemaphoreType.DMA((tall // (2 * CHUNK),)),
            pltpu.SemaphoreType.DMA((len(UNITS),)),
            pltpu.SemaphoreType.DMA((len(UNITS),)),
            pltpu.SemaphoreType.DMA((PEERS,)),
            pltpu.SemaphoreType.DMA((PEERS,)),
            pltpu.SemaphoreType.REGULAR,
        ],
        compiler_params=pltpu.CompilerParams(
            collective_id=0,
            has_side_effects=True,
        ),
    )(hidden, target_ids.reshape(count // 128, 128), owner, head.T)


def solution(mesh):
    return jax.shard_map(
        local,
        mesh=mesh,
        in_specs=(P(("dp", "vocab"), None), P("dp"), P("dp", None), P(None, "vocab")),
        out_specs=P(("dp", "vocab"), None),
        check_vma=False,
    )
```
